512 devices in a mesh: blk: 4 (over y), uly: 32 (over z, x_hi), dp: 4 (over x_lo, core).
Axes of the slice: x: 4 (x_hi: 2, x_lo: 2; x = x_hi * 2 + x_lo), y: 4, z: 16, core: 2. Of those that a mesh axis runs over, the one named last changes fastest.
Arguments:
- queries: bfloat16 [4, 16384, 4096], P(None, ('blk', 'uly', 'dp')), may hold values from -16 to 16
- keys: bfloat16 [4, 16384, 512], P(None, ('blk', 'uly', 'dp')), may hold values from -16 to 16
- values: bfloat16 [4, 16384, 512], P(None, ('blk', 'uly', 'dp')), may hold values from -6 to 6
- grad_out: bfloat16 [4, 16384, 4096], P(None, ('blk', 'uly', 'dp')), may hold values from -6 to 6
- segment_ids: int32 [4, 16384], replicated, may hold values from 0 to 63, never falling along the last dimension, each value on 1 to 512 neighbouring positions
- assignment: int32 [4], replicated, may hold values from 0 to 3, each once
Outputs:
- grad_queries: bfloat16 [4, 16384, 32, 128], P('dp', ('blk', 'uly'))
- grad_keys: bfloat16 [4, 16384, 512], P('dp', ('blk', 'uly'))
- grad_values: bfloat16 [4, 16384, 512], P('dp', ('blk', 'uly'))
The draws below stay inside these ranges and needn't reach their ends.
Inputs may be any that keep to these rules, and one draw needn't show every extreme that they name: `segment_ids`: no document holds more than 512 tokens, and some document holds exactly 512.
All inputs are finite; a program needn't handle non-finite values.
Results may differ from the reference program's by a relative error of at most 0.008.
Values may be sent and summed in bfloat16 or wider, within the bound.
A program may use at most 64 MiB of HBM per device.

```python
import math
import jax
import jax.numpy as jnp
import numpy as np
from jax import lax

QH = 32
KVH = 4
HD = 128
SEQS = 4
S = 16384
DOC_MAX = 512
DOCS = 64


def draw_queries(key, part):
    base = jnp.clip(jax.random.normal(jax.random.fold_in(key, 1), (SEQS, S, QH * HD), jnp.float32), -6.0, 6.0)
    return base.astype(jnp.bfloat16)


def draw_keys(key, part):
    base = jnp.clip(jax.random.normal(jax.random.fold_in(key, 2), (SEQS, S, KVH * HD), jnp.float32), -6.0, 6.0)
    return base.astype(jnp.bfloat16)


def block_levels(key, shape, split, low, high):
    def one(dim, parts):
        steps = jax.random.uniform(jax.random.fold_in(jax.random.fold_in(key, 6), dim), (parts,), jnp.float32, low / len(split), high / len(split))
        return jnp.repeat(jnp.exp(steps), shape[dim] // parts).reshape((-1,) + (1,) * (len(shape) - dim - 1))

    loudness = one(*split[0])
    for cut in split[1:]:
        loudness = loudness * one(*cut)
    return loudness


def length_profile(number_of, total, bound, skew):
    loads = [(1 << 20) // math.isqrt(rank ** skew) + 1 for rank in range(2, number_of + 1)]
    surplus, holding = total - bound - (number_of - 1), [1] * (number_of - 1)
    while surplus > 0:
        free = [i for i in range(number_of - 1) if holding[i] < bound]
        pool, budget = sum([loads[i] for i in free]), surplus
        for i in free:
            more = min(bound - holding[i], max(1, budget * loads[i] // pool), surplus)
            holding[i] = holding[i] + more
            surplus = surplus - more
    return np.array([bound] + holding)


def uneven(key, count, total, limit, lean):
    if count == 2:
        one = jax.random.randint(key, (), max(1, total - limit), min(limit, total - 1) + 1)
        return jnp.stack([one, total - one])
    sizes = jnp.asarray(length_profile(count, total, limit, lean), jnp.int32)
    couples = (count - 1) // 2
    giver, receiver = sizes[1:1 + 2 * couples:2], sizes[2:2 + 2 * couples:2]
    room = jnp.minimum(giver - 1, limit - receiver)
    moved = jax.random.randint(jax.random.fold_in(key, 1), (couples,), 0, 1 << 20) % (room + 1)
    sizes = sizes.at[1:1 + 2 * couples:2].set(giver - moved).at[2:2 + 2 * couples:2].set(receiver + moved)
    return sizes[jax.random.permutation(jax.random.fold_in(key, 2), count)]


def noise(key, dims, scale, reach, split=(), kind=jnp.bfloat16):
    result = jax.random.normal(key, dims, jnp.float32) * scale
    if len(split) > 0:
        result = block_levels(key, dims, split, -0.22, 0.18) * result
    return jnp.clip(result, min=-reach, max=reach).astype(kind)


def setup_inputs(seed: int = 0) -> dict:
    seeds = jax.random.split(jax.random.key(seed), 7)
    queries = draw_queries(jax.random.fold_in(seeds[6], 71), 0)
    keys = draw_keys(jax.random.fold_in(seeds[6], 71), 0)
    values = noise(seeds[2], (SEQS, S, KVH * HD), 1.0, 6.0, ((1, 512),))
    grad_out = noise(seeds[3], (SEQS, S, QH * HD), 1.0, 6.0, ((1, 512),))
    segment_ids = jax.vmap(lambda own: jnp.searchsorted(jnp.cumsum(uneven(own, DOCS, S, DOC_MAX, 2)), jnp.arange(S), side="right"))(jax.random.split(seeds[4], SEQS)).reshape((SEQS, S)).astype(jnp.int32)
    assignment = jax.random.permutation(seeds[5], SEQS).astype(jnp.int32)
    return dict(queries=queries, keys=keys, values=values, grad_out=grad_out, segment_ids=segment_ids, assignment=assignment)


def block_grads(query_block, grad_block, key_window, value_window, allowed, softmax_scale):
    scores = jnp.dot(query_block, key_window.T, preferred_element_type=jnp.float32) * softmax_scale
    scores = jnp.where(allowed, scores, -jnp.inf)
    top_score = jnp.max(scores, axis=1, keepdims=True)
    weights = jnp.where(allowed, jnp.exp(scores - top_score), 0.0)
    probs = weights / jnp.sum(weights, axis=1, keepdims=True)
    probs_half = probs.astype(jnp.bfloat16)
    grad_value = jnp.dot(probs_half.T, grad_block, preferred_element_type=jnp.float32)
    grad_probs = jnp.dot(grad_block, value_window.T, preferred_element_type=jnp.float32)
    row_delta = jnp.sum(probs * grad_probs, axis=1, keepdims=True)
    grad_scores = (softmax_scale * probs * (grad_probs - row_delta)).astype(jnp.bfloat16)
    grad_query = jnp.dot(grad_scores, key_window, preferred_element_type=jnp.float32).astype(jnp.bfloat16)
    grad_key = jnp.dot(grad_scores.T, query_block, preferred_element_type=jnp.float32)
    return grad_query, grad_key, grad_value


def head_grads(query_head, key_head, value_head, grad_head, segment_row):
    block_rows = DOC_MAX
    nblocks = S // block_rows
    softmax_scale = 1.0 / (HD ** 0.5)
    key_pad = jnp.concatenate([jnp.zeros((block_rows, HD), jnp.bfloat16), key_head], axis=0)
    value_pad = jnp.concatenate([jnp.zeros((block_rows, HD), jnp.bfloat16), value_head], axis=0)
    segment_pad = jnp.concatenate([jnp.full((block_rows,), -1, jnp.int32), segment_row.astype(jnp.int32)], axis=0)
    row_pos = jnp.arange(block_rows, dtype=jnp.int32) + block_rows
    col_pos = jnp.arange(2 * block_rows, dtype=jnp.int32)

    def step(carry, index):
        key_acc, value_acc = carry
        start = (index * block_rows).astype(jnp.int32)
        query_block = lax.dynamic_slice_in_dim(query_head, start, block_rows, 0)
        grad_block = lax.dynamic_slice_in_dim(grad_head, start, block_rows, 0)
        key_window = lax.dynamic_slice_in_dim(key_pad, start, 2 * block_rows, 0)
        value_window = lax.dynamic_slice_in_dim(value_pad, start, 2 * block_rows, 0)
        segment_query = lax.dynamic_slice_in_dim(segment_pad, start + block_rows, block_rows, 0)
        segment_key = lax.dynamic_slice_in_dim(segment_pad, start, 2 * block_rows, 0)
        allowed = (segment_query[:, None] == segment_key[None, :]) & (col_pos[None, :] <= row_pos[:, None])
        grad_query, grad_key, grad_value = block_grads(query_block, grad_block, key_window, value_window, allowed, softmax_scale)
        old_key = lax.dynamic_slice_in_dim(key_acc, start, 2 * block_rows, 0)
        old_value = lax.dynamic_slice_in_dim(value_acc, start, 2 * block_rows, 0)
        key_acc = lax.dynamic_update_slice_in_dim(key_acc, old_key + grad_key, start, 0)
        value_acc = lax.dynamic_update_slice_in_dim(value_acc, old_value + grad_value, start, 0)
        return (key_acc, value_acc), grad_query

    start_acc = jnp.zeros((S + block_rows, HD), jnp.float32)
    (key_acc, value_acc), grad_blocks = lax.scan(step, (start_acc, start_acc), jnp.arange(nblocks, dtype=jnp.int32))
    return grad_blocks.reshape(S, HD), key_acc[block_rows:], value_acc[block_rows:]


def one_sequence(query_seq, key_seq, value_seq, grad_seq, segment_row):
    group_size = QH // KVH
    query_split = query_seq.reshape(S, KVH, group_size, HD).transpose(1, 2, 0, 3)
    grad_split = grad_seq.reshape(S, KVH, group_size, HD).transpose(1, 2, 0, 3)
    key_split = key_seq.reshape(S, KVH, HD).transpose(1, 0, 2)
    value_split = value_seq.reshape(S, KVH, HD).transpose(1, 0, 2)

    def kv_group(items):
        query_group, grad_group, key_head, value_head = items

        def single(pair):
            return head_grads(pair[0], key_head, value_head, pair[1], segment_row)

        grad_query, grad_key, grad_value = lax.map(single, (query_group, grad_group))
        return grad_query, jnp.sum(grad_key, axis=0), jnp.sum(grad_value, axis=0)

    grad_query, grad_key, grad_value = lax.map(kv_group, (query_split, grad_split, key_split, value_split))
    grad_query = grad_query.transpose(2, 0, 1, 3).reshape(S, QH, HD)
    grad_key = grad_key.transpose(1, 0, 2).reshape(S, KVH * HD).astype(jnp.bfloat16)
    grad_value = grad_value.transpose(1, 0, 2).reshape(S, KVH * HD).astype(jnp.bfloat16)
    return grad_query, grad_key, grad_value


def reference(queries, keys, values, grad_out, segment_ids, assignment):
    query_list = []
    key_list = []
    value_list = []
    for group_index in range(SEQS):
        chosen = assignment[group_index]
        grad_query, grad_key, grad_value = one_sequence(queries[chosen], keys[chosen], values[chosen], grad_out[chosen], segment_ids[chosen])
        query_list.append(grad_query)
        key_list.append(grad_key)
        value_list.append(grad_value)
    return jnp.stack(query_list), jnp.stack(key_list), jnp.stack(value_list)
```

```python
import functools
import math

import jax
import jax.numpy as jnp
from jax import lax
from jax.experimental import pallas as pl
from jax.experimental.pallas import tpu as pltpu
from jax.sharding import PartitionSpec as P

KVH = 4
RATIO = 8
HD = 128
GROUPS = 4
PIECE = 32
TILE = 128
ROW = 256
WIN = 640
MESH = pl.DeviceIdType.MESH
NT = (((1,), (1,)), ((), ()))
NN = (((1,), (0,)), ((), ()))
MASKED = -1e30


def kernel(
    n_rows, z_rows,
    assign_ref, seg_ref, q_ref, do_ref, k_ref, v_ref,
    gq_ref, gk_ref, gv_ref,
    kvs, qds, kvb, qdb, bias, kt, part, a_out, a_in, b_out, b_in, own, c_out, c_in,
    kv_send, kv_recv, qd_send, qd_recv, f_send, f_recv, r_send, r_recv,
):
    blk = lax.axis_index("blk")
    uly = lax.axis_index("uly")
    d = lax.axis_index("dp")
    xh = uly % 2
    z = uly // 2
    row = blk * z_rows + z
    me = xh * GROUPS + d

    def in_row(member):
        return (blk, z * 2 + member // GROUPS, member % GROUPS)

    def in_column(other):
        return (other // z_rows, (other % z_rows) * 2 + xh, d)

    up = in_column((row + 1) % n_rows)
    down = in_column((row + n_rows - 1) % n_rows)
    across = (blk, z * 2 + (1 - xh), d)

    barrier = pltpu.get_barrier_semaphore()
    partners = [in_row((me + i) % 8) for i in range(1, 8)] + [up, down]
    for partner in partners:
        pl.semaphore_signal(barrier, inc=1, device_id=partner, device_id_type=MESH)

    for g in range(GROUPS):
        a = assign_ref[g]
        for h in range(KVH):
            cols = slice(h * HD, (h + 1) * HD)
            kvs[g, h, 0] = k_ref[a, :, cols]
            kvs[g, h, 1] = v_ref[a, :, cols]
    for g in range(GROUPS):
        a = assign_ref[g]
        for h in range(KVH):
            for r in range(RATIO):
                cols = slice((h * RATIO + r) * HD, (h * RATIO + r + 1) * HD)
                qds[g, h, 0, r] = q_ref[a, :, cols]
                qds[g, h, 1, r] = do_ref[a, :, cols]

    here = pl.ds(pl.multiple_of(d * PIECE, PIECE), PIECE)
    mine = pl.ds(pl.multiple_of(2 * ROW + me * PIECE, PIECE), PIECE)
    for h in range(KVH):
        kvb[h, :, mine, :] = kvs[d, h]

    pl.semaphore_wait(barrier, len(partners))

    def kv_copy(h, i):
        member = (me + i) % 8
        return pltpu.make_async_remote_copy(
            src_ref=kvs.at[member % GROUPS, h],
            dst_ref=kvb.at[h, :, mine, :],
            send_sem=kv_send.at[h, i - 1],
            recv_sem=kv_recv.at[h, i - 1],
            device_id=in_row(member),
            device_id_type=MESH,
        )

    def qd_copy(h, i):
        g = (d + i) % GROUPS
        return pltpu.make_async_remote_copy(
            src_ref=qds.at[g, h],
            dst_ref=qdb.at[h, :, :, here, :],
            send_sem=qd_send.at[h, i - 1],
            recv_sem=qd_recv.at[h, i - 1],
            device_id=(blk, uly, g),
            device_id_type=MESH,
        )

    def forward(h, step):
        return pltpu.make_async_remote_copy(
            src_ref=kvb.at[h, :, pl.ds((2 - step) * ROW, ROW), :],
            dst_ref=kvb.at[h, :, pl.ds((1 - step) * ROW, ROW), :],
            send_sem=f_send.at[h, step],
            recv_sem=f_recv.at[h, step],
            device_id=up,
            device_id_type=MESH,
        )

    def back(h, step):
        src, dst, device = (
            (a_out, a_in, down), (b_out, b_in, down), (c_out, c_in, across)
        )[step]
        return pltpu.make_async_remote_copy(
            src_ref=src.at[h],
            dst_ref=dst.at[h],
            send_sem=r_send.at[h, step],
            recv_sem=r_recv.at[h, step],
            device_id=device,
            device_id_type=MESH,
        )

    for h in range(KVH):
        for i in range(1, 8):
            kv_copy(h, i).start()
    for h in range(KVH):
        for i in (2, 1, 3):
            qd_copy(h, i).start()

    for h in range(KVH):
        for t in range(2):
            qdb[h, t, :, here, :] = qds[d, h, t]

    tile = row * 2 + xh
    n_tiles = n_rows * 2
    mine_seq = assign_ref[d]
    chosen = lax.broadcasted_iota(jnp.int32, (GROUPS, TILE), 0) == mine_seq

    def segments(t):
        cols = pl.ds(pl.multiple_of(t * TILE, TILE), TILE)
        ids = jnp.where(chosen, seg_ref[:, cols], 0).astype(jnp.float32)
        return jnp.broadcast_to(jnp.sum(ids, axis=0, keepdims=True), (TILE, TILE))

    of_query = segments(tile)
    for i in range(5):
        t = tile - 4 + i
        of_key = jnp.transpose(segments((t + n_tiles) % n_tiles))
        allowed = of_key == of_query
        if i < 4:
            shut = jnp.where(t < 0, MASKED, 0.0).astype(jnp.float32)
            bias[i * TILE:(i + 1) * TILE, :] = jnp.where(allowed, shut, MASKED)
        else:
            key_at = lax.broadcasted_iota(jnp.int32, (TILE, TILE), 0)
            query_at = lax.broadcasted_iota(jnp.int32, (TILE, TILE), 1)
            bias[i * TILE:(i + 1) * TILE, :] = jnp.where(
                allowed & (key_at <= query_at), 0.0, MASKED
            )
    part[...] = jnp.zeros_like(part)

    def pass_row(h):
        for i in range(1, 8):
            kv_copy(h, i).wait_recv()
        forward(h, 0).start()

    def pass_on(h):
        forward(h, 0).wait_recv()
        forward(h, 1).start()

    window = pl.ds(pl.multiple_of(xh * TILE, TILE), WIN)
    scale = 1.0 / math.sqrt(HD)
    to_log2 = scale * math.log2(math.e)

    def compute(h):
        kt[...] = jnp.transpose(kvb[h, 0, window, :].astype(jnp.float32)).astype(jnp.bfloat16)

        def pair(j, _):
            key = kvb[h, 0, window, :]
            value = kvb[h, 1, window, :]
            query = qdb[h, 0, pl.ds(2 * j, 2)].reshape(2 * TILE, HD)
            grad = qdb[h, 1, pl.ds(2 * j, 2)].reshape(2 * TILE, HD)
            shut = bias[...]
            scores = lax.dot_general(key, query, NT, preferred_element_type=jnp.float32)
            scores = scores * to_log2 + jnp.concatenate([shut, shut], axis=1)
            weights = jnp.exp2(scores - jnp.max(scores, axis=0, keepdims=True))
            probs = weights * (1.0 / jnp.sum(weights, axis=0, keepdims=True))
            grad_probs = lax.dot_general(value, grad, NT, preferred_element_type=jnp.float32)
            delta = jnp.sum(probs * grad_probs, axis=0, keepdims=True)
            grad_scores = (scale * probs * (grad_probs - delta)).astype(jnp.bfloat16)
            part[h, 1, window, :] += lax.dot_general(
                probs.astype(jnp.bfloat16), grad, NN, preferred_element_type=jnp.float32
            )
            part[h, 0, window, :] += lax.dot_general(
                grad_scores, query, NN, preferred_element_type=jnp.float32
            )
            grad_query = lax.dot_general(
                kt[...], grad_scores, NN, preferred_element_type=jnp.float32
            )
            for r in range(2):
                cols = pl.ds(pl.multiple_of((h * RATIO + 2 * j + r) * HD, HD), HD)
                gq_ref[:, cols] = jnp.transpose(
                    grad_query[:, r * TILE:(r + 1) * TILE]
                ).astype(jnp.bfloat16)
            return 0

        lax.fori_loop(0, RATIO // 2, pair, 0)
        a_out[h] = part[h, :, :ROW, :].astype(jnp.bfloat16)

    def add_first(h):
        back(h, 0).wait_recv()
        total = part[h, :, ROW:2 * ROW, :] + a_in[h].astype(jnp.float32)
        b_out[h] = total.astype(jnp.bfloat16)

    def add_second(h):
        back(h, 1).wait_recv()
        keep = pl.ds(pl.multiple_of(xh * TILE, TILE), TILE)
        give = pl.ds(pl.multiple_of((1 - xh) * TILE, TILE), TILE)
        keep_part = pl.ds(pl.multiple_of(2 * ROW + xh * TILE, TILE), TILE)
        give_part = pl.ds(pl.multiple_of(2 * ROW + (1 - xh) * TILE, TILE), TILE)
        c_out[h] = (part[h, :, give_part, :] + b_in[h, :, give, :].astype(jnp.float32)).astype(jnp.bfloat16)
        own[h] = part[h, :, keep_part, :] + b_in[h, :, keep, :].astype(jnp.float32)

    def finish(h):
        back(h, 2).wait_recv()
        total = (own[h] + c_in[h].astype(jnp.float32)).astype(jnp.bfloat16)
        cols = slice(h * HD, (h + 1) * HD)
        gk_ref[:, cols] = total[0]
        gv_ref[:, cols] = total[1]

    passed = 0
    for h in range(KVH):
        pass_row(h)
        if h >= 1 and passed < min(2, KVH):
            pass_on(passed)
            passed += 1
    for h in range(KVH):
        for i in range(1, 4):
            qd_copy(h, i).wait_recv()
        if passed <= h:
            pass_on(passed)
            passed += 1
        forward(h, 1).wait_recv()
        compute(h)
        if passed < KVH:
            pass_on(passed)
            passed += 1
        back(h, 0).start()
        if h >= 1:
            add_first(h - 1)
            back(h - 1, 1).start()
        if h >= 2:
            add_second(h - 2)
            back(h - 2, 2).start()
        if h >= 3:
            finish(h - 3)
    for h in range(KVH, KVH + 3):
        if 0 <= h - 1 < KVH:
            add_first(h - 1)
            back(h - 1, 1).start()
        if 0 <= h - 2 < KVH:
            add_second(h - 2)
            back(h - 2, 2).start()
        if 0 <= h - 3 < KVH:
            finish(h - 3)

    for h in range(KVH):
        for i in range(1, 8):
            kv_copy(h, i).wait_send()
        for i in range(1, 4):
            qd_copy(h, i).wait_send()
        for step in range(2):
            forward(h, step).wait_send()
        for step in range(3):
            back(h, step).wait_send()


def shards(n_rows, z_rows, queries, keys, values, grad_out, segment_ids, assignment):
    bf16, f32 = jnp.bfloat16, jnp.float32
    vmem = pl.BlockSpec(memory_space=pltpu.VMEM)
    dma = pltpu.SemaphoreType.DMA
    gq, gk, gv = pl.pallas_call(
        functools.partial(kernel, n_rows, z_rows),
        out_shape=(
            jax.ShapeDtypeStruct((TILE, KVH * RATIO * HD), bf16),
            jax.ShapeDtypeStruct((TILE, KVH * HD), bf16),
            jax.ShapeDtypeStruct((TILE, KVH * HD), bf16),
        ),
        in_specs=[pl.BlockSpec(memory_space=pltpu.SMEM)] + [vmem] * 5,
        out_specs=(vmem, vmem, vmem),
        scratch_shapes=[
            pltpu.VMEM((GROUPS, KVH, 2, PIECE, HD), bf16),
            pltpu.VMEM((GROUPS, KVH, 2, RATIO, PIECE, HD), bf16),
            pltpu.VMEM((KVH, 2, 3 * ROW, HD), bf16),
            pltpu.VMEM((KVH, 2, RATIO, TILE, HD), bf16),
            pltpu.VMEM((WIN, TILE), f32),
            pltpu.VMEM((HD, WIN), bf16),
            pltpu.VMEM((KVH, 2, 3 * ROW, HD), f32),
            pltpu.VMEM((KVH, 2, ROW, HD), bf16),
            pltpu.VMEM((KVH, 2, ROW, HD), bf16),
            pltpu.VMEM((KVH, 2, ROW, HD), bf16),
            pltpu.VMEM((KVH, 2, ROW, HD), bf16),
            pltpu.VMEM((KVH, 2, TILE, HD), f32),
            pltpu.VMEM((KVH, 2, TILE, HD), bf16),
            pltpu.VMEM((KVH, 2, TILE, HD), bf16),
            dma((KVH, 7)), dma((KVH, 7)),
            dma((KVH, 3)), dma((KVH, 3)),
            dma((KVH, 2)), dma((KVH, 2)),
            dma((KVH, 3)), dma((KVH, 3)),
        ],
        compiler_params=pltpu.CompilerParams(
            collective_id=0, has_side_effects=True, vmem_limit_bytes=60 * 1024 * 1024
        ),
        name="attention_backward",
    )(assignment, segment_ids, queries, grad_out, keys, values)
    return gq.reshape(1, TILE, KVH * RATIO, HD), gk[None], gv[None]


def solution(mesh):
    z_rows = mesh.shape["uly"] // 2
    n_rows = mesh.shape["blk"] * z_rows
    tokens = P(None, ("blk", "uly", "dp"), None)
    return jax.shard_map(
        functools.partial(shards, n_rows, z_rows),
        mesh=mesh,
        in_specs=(tokens, tokens, tokens, tokens, P(), P()),
        out_specs=(
            P("dp", ("blk", "uly"), None, None),
            P("dp", ("blk", "uly"), None),
            P("dp", ("blk", "uly"), None),
        ),
        check_vma=False,
    )
```

```python
import functools
import math

import jax
import jax.numpy as jnp
from jax import lax
from jax.experimental import pallas as pl
from jax.experimental.pallas import tpu as pltpu
from jax.sharding import PartitionSpec as P

KVH = 4
RATIO = 8
HD = 128
GROUPS = 4
PIECE = 32
TILE = 128
ROW = 256
WIN = 640
MESH = pl.DeviceIdType.MESH
NT = (((1,), (1,)), ((), ()))
NN = (((1,), (0,)), ((), ()))
MASKED = -1e30


def kernel(
    n_rows, z_rows,
    assign_hbm, seg_hbm, q_hbm, do_hbm, k_hbm, v_hbm,
    gq_ref, gk_ref, gv_ref,
    assign_ref, seg_ref, k_ref, v_ref, in_sem, kvs, qds, kvb, qdb, bias, kt, gq_part, part, a_out, a_in, b_out, b_in, own, c_out, c_in,
    kv_send, kv_recv, qd_send, qd_recv, f_send, f_recv, r_send, r_recv, x_send, x_recv, g_send, g_recv,
    *fetched,
):
    blk = lax.axis_index("blk")
    uly = lax.axis_index("uly")
    d = lax.axis_index("dp")
    xh = uly % 2
    z = uly // 2
    row = blk * z_rows + z
    me = xh * GROUPS + d

    def in_row(member):
        return (blk, z * 2 + member // GROUPS, member % GROUPS)

    def in_column(other):
        return (other // z_rows, (other % z_rows) * 2 + xh, d)

    up = in_column((row + 1) % n_rows)
    down = in_column((row + n_rows - 1) % n_rows)
    across = (blk, z * 2 + (1 - xh), d)
    up_across = (up[0], up[1] + 1 - 2 * xh, d)
    down_across = (down[0], down[1] + 1 - 2 * xh, d)

    def fetch_keys():
        return [
            pltpu.make_async_copy(k_hbm, k_ref, in_sem.at[0]),
            pltpu.make_async_copy(v_hbm, v_ref, in_sem.at[1]),
        ]

    def fetch_queries(h):
        cols = pl.ds(h * RATIO * HD, RATIO * HD)
        return [
            pltpu.make_async_copy(src.at[:, :, cols], fetched[2 * h + i], in_sem.at[3 + 2 * h + i])
            for i, src in enumerate((q_hbm, do_hbm))
        ]

    fetch_assignment = pltpu.make_async_copy(assign_hbm, assign_ref, in_sem.at[3 + 2 * KVH])
    fetch_assignment.start()
    fetch_segments = pltpu.make_async_copy(seg_hbm, seg_ref, in_sem.at[2])
    for copy in fetch_keys():
        copy.start()
    for h in range(KVH):
        for copy in fetch_queries(h):
            copy.start()
    fetch_segments.start()

    barrier = pltpu.get_barrier_semaphore()
    partners = [in_row((me + i) % 8) for i in range(1, 8)] + [up, down, up_across, down_across]
    for partner in partners:
        pl.semaphore_signal(barrier, inc=1, device_id=partner, device_id_type=MESH)

    def stage_keys(h):
        cols = slice(h * HD, (h + 1) * HD)
        for g in range(GROUPS):
            a = assign_ref[g]
            kvs[g, h, 0] = k_ref[a, :, cols]
            kvs[g, h, 1] = v_ref[a, :, cols]

    def stage_queries(h):
        for copy in fetch_queries(h):
            copy.wait()
        for g in range(GROUPS):
            a = assign_ref[g]
            for r in range(RATIO):
                cols = slice(r * HD, (r + 1) * HD)
                qds[g, h, 0, r] = fetched[2 * h][a, :, cols]
                qds[g, h, 1, r] = fetched[2 * h + 1][a, :, cols]

    fetch_assignment.wait()
    for copy in fetch_keys():
        copy.wait()
    for h in range(KVH):
        stage_keys(h)
    stage_queries(0)

    here = pl.ds(pl.multiple_of(d * PIECE, PIECE), PIECE)
    mine = pl.ds(pl.multiple_of(2 * ROW + me * PIECE, PIECE), PIECE)
    for h in range(KVH):
        kvb[h, :, mine, :] = kvs[d, h]

    pl.semaphore_wait(barrier, len(partners))

    def kv_copy(h, i):
        member = (me + i) % 8
        return pltpu.make_async_remote_copy(
            src_ref=kvs.at[member % GROUPS, h],
            dst_ref=kvb.at[h, :, mine, :],
            send_sem=kv_send.at[h, i - 1],
            recv_sem=kv_recv.at[h, i - 1],
            device_id=in_row(member),
            device_id_type=MESH,
        )

    def qd_copy(h, j, i):
        g = (d + i) % GROUPS
        heads = pl.ds(2 * j, 2)
        return pltpu.make_async_remote_copy(
            src_ref=qds.at[g, h, :, heads],
            dst_ref=qdb.at[h, :, heads, here, :],
            send_sem=qd_send.at[h, j, i - 1],
            recv_sem=qd_recv.at[h, j, i - 1],
            device_id=(blk, uly, g),
            device_id_type=MESH,
        )

    def forward(h, step):
        return pltpu.make_async_remote_copy(
            src_ref=kvb.at[h, :, pl.ds((2 - step) * ROW, ROW), :],
            dst_ref=kvb.at[h, :, pl.ds((1 - step) * ROW, ROW), :],
            send_sem=f_send.at[h, step],
            recv_sem=f_recv.at[h, step],
            device_id=up,
            device_id_type=MESH,
        )

    keep = pl.ds(pl.multiple_of(xh * TILE, TILE), TILE)
    give = pl.ds(pl.multiple_of((1 - xh) * TILE, TILE), TILE)

    def direct(h):
        return h == KVH - 1

    def back(h, step, t):
        src, dst, device = ((a_out, a_in, down), (b_out, b_in, down))[step]
        rows = (give, keep)[t]
        if direct(h) and step == 1 and t == 0:
            return pltpu.make_async_remote_copy(
                src_ref=b_out.at[h, :, give, :],
                dst_ref=b_in.at[h, :, keep, :],
                send_sem=g_send,
                recv_sem=g_recv,
                device_id=down_across,
                device_id_type=MESH,
            )
        return pltpu.make_async_remote_copy(
            src_ref=src.at[h, :, rows, :],
            dst_ref=dst.at[h, :, rows, :],
            send_sem=r_send.at[h, step, t],
            recv_sem=r_recv.at[h, step, t],
            device_id=device,
            device_id_type=MESH,
        )

    def cross(h):
        return pltpu.make_async_remote_copy(
            src_ref=c_out.at[h],
            dst_ref=c_in.at[h],
            send_sem=x_send.at[h],
            recv_sem=x_recv.at[h],
            device_id=across,
            device_id_type=MESH,
        )

    def send_keys(h):
        for i in range(1, 8):
            kv_copy(h, i).start()

    def send_queries(h):
        for j in range(RATIO // 2):
            for i in (2, 1, 3):
                qd_copy(h, j, i).start()

    send_keys(0)
    send_keys(1)
    stage_queries(1)
    send_queries(0)
    send_keys(2)
    send_keys(3)
    stage_queries(2)
    send_queries(1)
    stage_queries(3)
    send_queries(2)
    send_queries(3)

    for h in range(KVH):
        for t in range(2):
            qdb[h, t, :, here, :] = qds[d, h, t]

    fetch_segments.wait()
    tile = row * 2 + xh
    n_tiles = n_rows * 2
    mine_seq = assign_ref[d]
    chosen = lax.broadcasted_iota(jnp.int32, (GROUPS, TILE), 0) == mine_seq

    def segments(t):
        cols = pl.ds(pl.multiple_of(t * TILE, TILE), TILE)
        ids = jnp.where(chosen, seg_ref[:, cols], 0).astype(jnp.float32)
        return jnp.broadcast_to(jnp.sum(ids, axis=0, keepdims=True), (TILE, TILE))

    of_query = segments(tile)
    for i in range(5):
        t = tile - 4 + i
        of_key = jnp.transpose(segments((t + n_tiles) % n_tiles))
        allowed = of_key == of_query
        if i < 4:
            shut = jnp.where(t < 0, MASKED, 0.0).astype(jnp.float32)
            bias[i * TILE:(i + 1) * TILE, :] = jnp.where(allowed, shut, MASKED)
        else:
            key_at = lax.broadcasted_iota(jnp.int32, (TILE, TILE), 0)
            query_at = lax.broadcasted_iota(jnp.int32, (TILE, TILE), 1)
            bias[i * TILE:(i + 1) * TILE, :] = jnp.where(
                allowed & (key_at <= query_at), 0.0, MASKED
            )
    part[...] = jnp.zeros_like(part)

    def pass_row(h):
        for i in range(1, 8):
            kv_copy(h, i).wait_recv()
        forward(h, 0).start()

    def pass_on(h):
        forward(h, 0).wait_recv()
        forward(h, 1).start()

    window = pl.ds(pl.multiple_of(xh * TILE, TILE), WIN)
    scale = 1.0 / math.sqrt(HD)
    to_log2 = scale * math.log2(math.e)

    def compute(h, first, last):
        if first == 0:
            forward(h, 1).wait_recv()
            kt[...] = jnp.transpose(
                kvb[h, 0, window, :].astype(jnp.float32)
            ).astype(jnp.bfloat16)

        def pair(j, _):
            for i in range(1, 4):
                qd_copy(h, j, i).wait_recv()
            key = kvb[h, 0, window, :]
            value = kvb[h, 1, window, :]
            query = qdb[h, 0, pl.ds(2 * j, 2)].reshape(2 * TILE, HD)
            grad = qdb[h, 1, pl.ds(2 * j, 2)].reshape(2 * TILE, HD)
            shut = bias[...]
            scores = lax.dot_general(key, query, NT, preferred_element_type=jnp.float32)
            scores = scores * to_log2 + jnp.concatenate([shut, shut], axis=1)
            weights = jnp.exp2(scores - jnp.max(scores, axis=0, keepdims=True))
            probs = weights * (1.0 / jnp.sum(weights, axis=0, keepdims=True))
            grad_probs = lax.dot_general(value, grad, NT, preferred_element_type=jnp.float32)
            delta = jnp.sum(probs * grad_probs, axis=0, keepdims=True)
            grad_scores = (scale * probs * (grad_probs - delta)).astype(jnp.bfloat16)
            part[h, 1, window, :] += lax.dot_general(
                probs.astype(jnp.bfloat16), grad, NN, preferred_element_type=jnp.float32
            )
            part[h, 0, window, :] += lax.dot_general(
                grad_scores, query, NN, preferred_element_type=jnp.float32
            )
            grad_query = lax.dot_general(
                kt[...], grad_scores, NN, preferred_element_type=jnp.float32
            )
            for r in range(2):
                head = h * RATIO + 2 * j + r
                gq_part[pl.ds(head, TILE, stride=KVH * RATIO), :] = jnp.transpose(
                    grad_query[:, r * TILE:(r + 1) * TILE]
                )
            return 0

        lax.fori_loop(first, last, pair, 0)

    keep_at = pl.ds(pl.multiple_of(2 * ROW + xh * TILE, TILE), TILE)
    give_at = pl.ds(pl.multiple_of(2 * ROW + (1 - xh) * TILE, TILE), TILE)

    def start_return(h):
        a_out[h] = part[h, :, :ROW, :].astype(jnp.bfloat16)
        if direct(h):
            c_out[h] = part[h, :, give_at, :].astype(jnp.bfloat16)
        for t in range(2):
            back(h, 0, t).start()
        if direct(h):
            cross(h).start()

    def add_first(h):
        for t, rows in enumerate((give, keep)):
            back(h, 0, t).wait_recv()
            offset = (1 - xh) if t == 0 else xh
            at = pl.ds(pl.multiple_of(ROW + offset * TILE, TILE), TILE)
            total = part[h, :, at, :] + a_in[h, :, rows, :].astype(jnp.float32)
            b_out[h, :, rows, :] = total.astype(jnp.bfloat16)
            back(h, 1, t).start()

    def add_second(h):
        if not direct(h):
            back(h, 1, 0).wait_recv()
            total = part[h, :, give_at, :] + b_in[h, :, give, :].astype(jnp.float32)
            c_out[h] = total.astype(jnp.bfloat16)
            cross(h).start()
        back(h, 1, 1).wait_recv()
        own[h] = part[h, :, keep_at, :] + b_in[h, :, keep, :].astype(jnp.float32)

    def finish(h):
        cross(h).wait_recv()
        total = own[h] + c_in[h].astype(jnp.float32)
        if direct(h):
            back(h, 1, 0).wait_recv()
            total += b_in[h, :, give, :].astype(jnp.float32)
        total = total.astype(jnp.bfloat16)
        cols = slice(h * HD, (h + 1) * HD)
        gk_ref[:, cols] = total[0]
        gv_ref[:, cols] = total[1]

    def write_queries(h):
        heads = gq_part[...].reshape(TILE, KVH * RATIO, HD)
        part_of = slice((h - 1) * RATIO, (h + 1) * RATIO)
        gq_ref[0, :, part_of, :] = heads[:, part_of, :].astype(jnp.bfloat16)

    pairs = RATIO // 2
    pass_row(0)
    pass_row(1)
    pass_on(0)
    pass_on(1)
    pass_row(2)
    compute(0,0,1)
    pass_row(3)
    compute(0,1,pairs)
    start_return(0)
    compute(1,0,2)
    pass_on(2)
    compute(1,2,pairs)
    start_return(1)
    add_first(0)
    pass_on(3)
    write_queries(1)
    compute(2,0,2)
    add_first(1)
    add_second(0)
    compute(2,2,pairs)
    start_return(2)
    finish(0)
    compute(3,0,2)
    add_second(1)
    compute(3,2,3)
    add_first(2)
    compute(3,3,pairs)
    start_return(3)
    write_queries(3)
    finish(1)
    add_first(3)
    add_second(2)
    finish(2)
    add_second(3)
    finish(3)

    for h in range(KVH):
        for i in range(1, 8):
            kv_copy(h, i).wait_send()
        for j in range(RATIO // 2):
            for i in range(1, 4):
                qd_copy(h, j, i).wait_send()
        for step in range(2):
            forward(h, step).wait_send()
            for t in range(2):
                back(h, step, t).wait_send()
        cross(h).wait_send()


def write_out(gq_ref, gk_ref, gv_ref, gq_out, gk_out, gv_out, sem):
    copies = [
        pltpu.make_async_copy(gq_ref, gq_out, sem.at[0]),
        pltpu.make_async_copy(gk_ref, gk_out.at[0], sem.at[1]),
        pltpu.make_async_copy(gv_ref, gv_out.at[0], sem.at[2]),
    ]
    for copy in copies:
        copy.start()
    for copy in copies:
        copy.wait()


def shards(n_rows, z_rows, queries, keys, values, grad_out, segment_ids, assignment):
    bf16, f32 = jnp.bfloat16, jnp.float32
    vmem = pl.BlockSpec(memory_space=pltpu.VMEM)
    dma = pltpu.SemaphoreType.DMA
    gq, gk, gv = pl.pallas_call(
        functools.partial(kernel, n_rows, z_rows),
        out_shape=(
            jax.ShapeDtypeStruct((1, TILE, KVH * RATIO, HD), bf16),
            jax.ShapeDtypeStruct((TILE, KVH * HD), bf16),
            jax.ShapeDtypeStruct((TILE, KVH * HD), bf16),
        ),
        in_specs=[pl.BlockSpec(memory_space=pltpu.HBM)] * 6,
        out_specs=(vmem, vmem, vmem),
        scratch_shapes=[
            pltpu.SMEM((GROUPS,), jnp.int32),
            pltpu.VMEM(segment_ids.shape, jnp.int32),
            pltpu.VMEM(keys.shape, bf16),
            pltpu.VMEM(keys.shape, bf16),
            dma((4 + 2 * KVH,)),
            pltpu.VMEM((GROUPS, KVH, 2, PIECE, HD), bf16),
            pltpu.VMEM((GROUPS, KVH, 2, RATIO, PIECE, HD), bf16),
            pltpu.VMEM((KVH, 2, 3 * ROW, HD), bf16),
            pltpu.VMEM((KVH, 2, RATIO, TILE, HD), bf16),
            pltpu.VMEM((WIN, TILE), f32),
            pltpu.VMEM((HD, WIN), bf16),
            pltpu.VMEM((TILE * KVH * RATIO, HD), f32),
            pltpu.VMEM((KVH, 2, 3 * ROW, HD), f32),
            pltpu.VMEM((KVH, 2, ROW, HD), bf16),
            pltpu.VMEM((KVH, 2, ROW, HD), bf16),
            pltpu.VMEM((KVH, 2, ROW, HD), bf16),
            pltpu.VMEM((KVH, 2, ROW, HD), bf16),
            pltpu.VMEM((KVH, 2, TILE, HD), f32),
            pltpu.VMEM((KVH, 2, TILE, HD), bf16),
            pltpu.VMEM((KVH, 2, TILE, HD), bf16),
            dma((KVH, 7)), dma((KVH, 7)),
            dma((KVH, RATIO // 2, 3)), dma((KVH, RATIO // 2, 3)),
            dma((KVH, 2)), dma((KVH, 2)),
            dma((KVH, 2, 2)), dma((KVH, 2, 2)),
            dma((KVH,)), dma((KVH,)), dma(()), dma(()),
        ]
        + [pltpu.VMEM((GROUPS, PIECE, RATIO * HD), bf16)] * (2 * KVH),
        compiler_params=pltpu.CompilerParams(
            collective_id=0, has_side_effects=True, vmem_limit_bytes=32 * 1024 * 1024
        ),
        name="attention_backward",
    )(
        *(
            pltpu.with_memory_space_constraint(array, pltpu.HBM)
            for array in (assignment, segment_ids, queries, grad_out, keys, values)
        )
    )
    return pl.pallas_call(
        write_out,
        out_shape=(
            jax.ShapeDtypeStruct(gq.shape, bf16),
            jax.ShapeDtypeStruct((1,) + gk.shape, bf16),
            jax.ShapeDtypeStruct((1,) + gv.shape, bf16),
        ),
        in_specs=[vmem] * 3,
        out_specs=[pl.BlockSpec(memory_space=pl.ANY)] * 3,
        scratch_shapes=[dma((3,))],
        compiler_params=pltpu.CompilerParams(vmem_limit_bytes=4 * 1024 * 1024),
        name="write_out",
    )(gq, gk, gv)


def solution(mesh):
    z_rows = mesh.shape["uly"] // 2
    n_rows = mesh.shape["blk"] * z_rows
    tokens = P(None, ("blk", "uly", "dp"), None)
    return jax.shard_map(
        functools.partial(shards, n_rows, z_rows),
        mesh=mesh,
        in_specs=(tokens, tokens, tokens, tokens, P(), P()),
        out_specs=(
            P("dp", ("blk", "uly"), None, None),
            P("dp", ("blk", "uly"), None),
            P("dp", ("blk", "uly"), None),
        ),
        check_vma=False,
    )
```
